32 devices in a mesh: gx: 4 (over y, x), gy: 8 (over z, core).
Axes of the slice: x: 2, y: 2, z: 4, core: 2. Of those that a mesh axis runs over, the one named last changes fastest.
Arguments:
- schur: float32 [4, 8, 512, 512], P('gx', 'gy'), may hold values from -1 to 25, as said below
- precond: float32 [4, 8, 512, 512], P('gx', 'gy'), may hold values from -1 to 25, as said below
- loads: float32 [4, 8, 512, 256], P('gx', 'gy'), may hold values from -12 to 12
- coarse_inv: float32 [128, 128], P('gx'), may hold values from -1 to 25, as said below
- edge_rows: int32 [4, 8, 512], P('gx', 'gy'), may hold values from 0 to 511, each once within a row
- corner_rows: int32 [4, 8, 4], P('gx', 'gy'), may hold values from 0 to 511, as said below
Outputs:
- multipliers: float32 [4, 8, 512, 256], P('gx', 'gy')
- residual: float32 [4, 8, 512, 256], P('gx', 'gy')
The draws below stay inside these ranges and needn't reach their ends.
Inputs may be any that keep to these rules, and one draw needn't show every extreme that they name: `edge_rows`: for every subdomain the 512 entries name each local interface row once. `corner_rows`: local interface rows of each subdomain's 4 corner modes; entries of one subdomain may repeat. `schur`: every subdomain's block is symmetric positive definite. `precond`: every subdomain's block is symmetric positive definite. `coarse_inv`: symmetric positive definite; row and column (i * 8 + j) * 4 + m belong to mode m of subdomain (i, j).
All inputs are finite; a program needn't handle non-finite values.
Results may differ from the reference program's by a relative error of at most 0.00017.
Values sent between devices are 32-bit elements; how exact they have to be, the bound alone decides.
No kernel may reach another device: no remote copies, remote signals or barrier semaphores. Data moves between devices by JAX's collectives and lax.ppermute only.
A program may use at most 64 MiB of HBM per device.

```python
import math
import jax
import jax.numpy as jnp
from jax import lax

EDGE = 128
MODES = 4
ITERS = 2
CASES = 256
SX = 4
SY = 8
IFACE = 512
COARSE = 128


def spd_block(key, order):
    first_key = jax.random.fold_in(key, 1)
    second_key = jax.random.fold_in(key, 2)
    diagonal = jnp.exp(jax.random.uniform(first_key, (order,), minval=0.0, maxval=math.log(2.5)))
    raw_part = jax.random.uniform(second_key, (order, order), minval=-1.0, maxval=1.0) * (0.8 / math.sqrt(order))
    return jnp.diag(diagonal) + 0.5 * (raw_part + raw_part.T)


def spd_stack(key, salt):
    count_sub = SX * SY
    keys = jax.random.split(jax.random.fold_in(key, salt), count_sub)
    blocks = jax.vmap(lambda single: spd_block(single, IFACE))(keys)
    return blocks.reshape(SX, SY, IFACE, IFACE)


def draw_schur(key, part):
    return spd_stack(key, 11)


def draw_precond(key, part):
    return spd_stack(key, 13)


def draw_coarse_inv(key, part):
    matrix = spd_block(jax.random.fold_in(key, 17), COARSE)
    return matrix


def draw_loads(key, part):
    count_sub = SX * SY
    rising = 0.6 + 1.2 * jnp.arange(count_sub, dtype=jnp.float32) / max(count_sub - 1, 1)
    base = jnp.clip(jax.random.normal(jax.random.fold_in(key, 21), (count_sub, IFACE, CASES)), -4.0, 4.0)
    values = base * rising[:, None, None]
    return values.reshape(SX, SY, IFACE, CASES)


def draw_corner_rows(key, part):
    drawn = jax.random.randint(jax.random.fold_in(key, 31), (SX, SY, MODES), 0, IFACE)
    drawn = drawn.at[0, 0, 0].set(IFACE - 1)
    drawn = drawn.at[0, 0, 1].set(0)
    return drawn.astype(jnp.int32)


def setup_inputs(seed: int = 0) -> dict:
    seeds = jax.random.split(jax.random.key(seed), 7)
    schur = draw_schur(jax.random.fold_in(seeds[6], 71), 0)
    precond = draw_precond(jax.random.fold_in(seeds[6], 71), 0)
    loads = draw_loads(jax.random.fold_in(seeds[6], 71), 0)
    coarse_inv = draw_coarse_inv(jax.random.fold_in(seeds[6], 71), 0)
    edge_rows = jax.vmap(lambda own: jax.random.permutation(own, IFACE))(jax.random.split(seeds[4], SX * SY)).reshape((SX, SY, IFACE)).astype(jnp.int32)
    corner_rows = draw_corner_rows(jax.random.fold_in(seeds[6], 71), 0)
    return {"schur": schur, "precond": precond, "loads": loads, "coarse_inv": coarse_inv, "edge_rows": edge_rows, "corner_rows": corner_rows}


highest = lax.Precision.HIGHEST


def inverse_rows(edge_rows):
    def invert_single(rows):
        return jnp.zeros((IFACE,), jnp.int32).at[rows].set(jnp.arange(IFACE, dtype=jnp.int32))
    return jax.vmap(jax.vmap(invert_single))(edge_rows)


def edge_jumps(source, edge_rows, inverse):
    index_full = jnp.broadcast_to(edge_rows[..., None], (SX, SY, IFACE, CASES))
    picked = jnp.take_along_axis(source, index_full, axis=2).reshape(SX, SY, 4, EDGE, CASES)
    west_jump = picked[:, :, 0] - jnp.roll(picked[:, :, 1], 1, axis=0)
    east_jump = picked[:, :, 1] - jnp.roll(picked[:, :, 0], -1, axis=0)
    south_jump = picked[:, :, 2] - jnp.roll(picked[:, :, 3], 1, axis=1)
    north_jump = picked[:, :, 3] - jnp.roll(picked[:, :, 2], -1, axis=1)
    stacked = jnp.stack([west_jump, east_jump, south_jump, north_jump], axis=2).reshape(SX, SY, IFACE, CASES)
    back_index = jnp.broadcast_to(inverse[..., None], (SX, SY, IFACE, CASES))
    return jnp.take_along_axis(stacked, back_index, axis=2)


def reference(schur, precond, loads, coarse_inv, edge_rows, corner_rows):
    inverse = inverse_rows(edge_rows)
    corner_pick = (corner_rows[..., None] == jnp.arange(IFACE, dtype=jnp.int32)).astype(jnp.float32)
    dual_rhs = edge_jumps(loads, edge_rows, inverse)
    multipliers = jnp.zeros((SX, SY, IFACE, CASES), jnp.float32)
    residual = dual_rhs
    for iteration in range(ITERS):
        coarse_res = jnp.einsum("abmi,abic->abmc", corner_pick, residual, precision=highest).reshape(COARSE, CASES)
        coarse_sol = jnp.dot(coarse_inv, coarse_res, precision=highest, preferred_element_type=jnp.float32)
        coarse_sol = coarse_sol.reshape(SX, SY, MODES, CASES)
        lifted = 0.25 * jnp.einsum("abij,abjc->abic", precond, residual, precision=highest)
        lifted = lifted + jnp.einsum("abmi,abmc->abic", corner_pick, coarse_sol, precision=highest)
        search = edge_jumps(lifted, edge_rows, inverse)
        schur_image = jnp.einsum("abij,abjc->abic", schur, search, precision=highest)
        dual_image = edge_jumps(schur_image, edge_rows, inverse)
        step_size = jnp.sum(residual * search, axis=(0, 1, 2)) / jnp.sum(search * dual_image, axis=(0, 1, 2))
        multipliers = multipliers + step_size * search
        residual = residual - step_size * dual_image
    return multipliers, residual
```

```python
import jax
import jax.numpy as jnp
from jax import lax
from jax.experimental import pallas as pl
from jax.experimental.pallas import tpu as pltpu
from jax.sharding import PartitionSpec as P

ITERS = 2
F32 = jnp.float32
BF16 = jnp.bfloat16
SUBLANES = 8


def halves(x):
    high = x.astype(BF16)
    return high, (x - high.astype(F32)).astype(BF16)


def thirds(x):
    high, rest = x.astype(BF16), None
    rest = x - high.astype(F32)
    middle, low = halves(rest)
    return high, middle, low


def dot(a, b):
    return jnp.dot(a, b, preferred_element_type=F32)


def dot_split(a_high, a_low, b):
    b_high, b_low = halves(b)
    return dot(a_high, b_high) + (dot(a_high, b_low) + dot(a_low, b_high))


def dot_exact(pick, x):
    high, middle, low = thirds(x)
    return dot(pick, high) + (dot(pick, middle) + dot(pick, low))


def one_hot_rows(rows_col, order):
    lanes = lax.broadcasted_iota(jnp.int32, (rows_col.shape[0], order), 1)
    return (rows_col == lanes).astype(F32).astype(BF16)


def one_hot_cols(rows_row, order):
    sublanes = lax.broadcasted_iota(jnp.int32, (order, rows_row.shape[1]), 0)
    return (rows_row == sublanes).astype(F32).astype(BF16)


def call(body, name, outs, args, flops=0, scalars=()):
    vmem = pl.BlockSpec(memory_space=pltpu.VMEM)
    smem = pl.BlockSpec(memory_space=pltpu.SMEM)
    moved = sum(a.size * a.dtype.itemsize for a in args)
    return pl.pallas_call(
        body,
        name=name,
        out_shape=[jax.ShapeDtypeStruct(s, d) for s, d in outs],
        in_specs=[smem] * len(scalars) + [vmem] * len(args),
        out_specs=[vmem] * len(outs),
        cost_estimate=pl.CostEstimate(flops=flops, bytes_accessed=moved, transcendentals=0),
        compiler_params=pltpu.CompilerParams(vmem_limit_bytes=24 * 1024 * 1024),
    )(*scalars, *args)


def gather_body(modes, edge, cases):
    def body(place, rows_col, corner_col, rows_row, loads, coarse, *outs):
        payloads, corner_out = outs[:4], outs[4]
        order = loads.shape[0]
        moved = dot_exact(one_hot_rows(rows_col[...], order), loads[...])
        corner = (corner_col[...] == rows_row[...]).astype(F32)
        corner_out[...] = corner
        own = [coarse[pl.ds(place[0] * modes + m, 1), :] for m in range(modes)]
        own = jnp.concatenate(own, axis=0)
        for k, out in enumerate(payloads):
            out[:edge, :] = moved[k * edge : (k + 1) * edge]
            info = jnp.concatenate([corner[:modes, k * edge : (k + 1) * edge], own], axis=1)
            for g in range((out.shape[0] - edge) // SUBLANES):
                part = info[:, g * cases : (g + 1) * cases]
                out[edge + g * SUBLANES : edge + g * SUBLANES + modes, : part.shape[1]] = part
    return body


def permute_body(rows_col, rows_row, block, high_out, low_out):
    order = block.shape[0]
    left = one_hot_rows(rows_col[...], order)
    right = one_hot_cols(rows_row[...], order)
    for part, out in zip(halves(block[...]), (high_out, low_out)):
        out[...] = dot(left, dot(part, right).astype(BF16)).astype(BF16)


def coarse_body(modes, edge, cases, devices):
    def body(mine0, mine1, mine2, mine3, his0, his1, his2, his3, high_out, low_out):
        total = devices * modes

        def info(ref):
            groups = (ref.shape[0] - edge) // SUBLANES
            parts = [
                ref[edge + g * SUBLANES : edge + g * SUBLANES + modes, :] for g in range(groups)
            ]
            whole = jnp.concatenate(parts, axis=1)
            return whole[:, :edge], whole[:, edge : edge + total]

        before = lax.broadcasted_iota(jnp.int32, (total, total), 0)
        after = lax.broadcasted_iota(jnp.int32, (total, total), 1)
        mode = jnp.zeros_like(after)
        for m in range(1, modes):
            mode = mode + (after >= m * devices).astype(jnp.int32)
        shuffle = (before == (after - mode * devices) * modes + mode).astype(F32).astype(BF16)
        for k, (mine, his) in enumerate(zip((mine0, mine1, mine2, mine3), (his0, his1, his2, his3))):
            my_pick, my_rows = info(mine)
            his_pick, his_rows = info(his)
            picks = jnp.concatenate([my_pick, -his_pick], axis=0).astype(BF16)
            rows = jnp.concatenate([my_rows, his_rows], axis=0)
            shuffled = dot_exact_right(rows, shuffle)
            high, low = [], None
            spread = sum(
                lax.dot_general(
                    picks, part, (((0,), (0,)), ((), ())), preferred_element_type=F32
                )
                for part in thirds(shuffled)
            )
            high, low = halves(spread)
            high_out[k * edge : (k + 1) * edge, :] = high
            low_out[k * edge : (k + 1) * edge, :] = low
    return body


def dot_exact_right(x, pick):
    high, middle, low = thirds(x)
    return dot(high, pick) + (dot(middle, pick) + dot(low, pick))


def solution(mesh):
    across, along = mesh.shape["gx"], mesh.shape["gy"]
    devices = across * along
    axes = ("gx", "gy")

    def ring_pairs(count, odd):
        pairs = []
        for first in range(odd, count + odd, 2):
            a, b = first % count, (first + 1) % count
            pairs += [(a, b), (b, a)]
        return pairs

    routes = (
        ("gx", ring_pairs(across, 0)),
        ("gx", ring_pairs(across, 1)),
        ("gy", ring_pairs(along, 0)),
        ("gy", ring_pairs(along, 1)),
    )

    def swap(parts):
        return [lax.ppermute(part, axis, pairs) for part, (axis, pairs) in zip(parts, routes)]

    def to_all(x):
        return lax.all_to_all(x, axes, 0, 0)

    def on_device(schur, precond, loads, coarse_inv, edge_rows, corner_rows):
        schur, precond, loads = schur[0, 0], precond[0, 0], loads[0, 0]
        order, cases = loads.shape
        modes = corner_rows.shape[2]
        edge = order // 4
        i, j = lax.axis_index("gx"), lax.axis_index("gy")
        west, east, south, north = jnp.split(edge_rows[0, 0], 4)
        even_i, even_j = i % 2 == 0, j % 2 == 0
        rows = jnp.concatenate(
            [
                jnp.where(even_i, east, west),
                jnp.where(even_i, west, east),
                jnp.where(even_j, north, south),
                jnp.where(even_j, south, north),
            ]
        )
        rows_col, rows_row = rows[:, None], rows[None, :]
        corner_col = jnp.concatenate(
            [corner_rows[0, 0], jnp.full((SUBLANES - modes,), -1, jnp.int32)]
        )[:, None]
        place = j.astype(jnp.int32).reshape(1)
        total = devices * modes
        groups = -(-(edge + total) // cases)
        payload_rows = edge + groups * SUBLANES
        mat = 2 * order * order * cases

        *payloads, corner = call(
            gather_body(modes, edge, cases),
            "gather",
            [((payload_rows, cases), F32)] * 4 + [((SUBLANES, order), F32)],
            (rows_col, corner_col, rows_row, loads, coarse_inv),
            3 * mat,
            (place,),
        )
        got = swap(payloads)
        pre_high, pre_low = call(
            permute_body, "permute_precond", [((order, order), BF16)] * 2,
            (rows_col, rows_row, precond), 8 * order**3,
        )
        sch_high, sch_low = call(
            permute_body, "permute_schur", [((order, order), BF16)] * 2,
            (rows_col, rows_row, schur), 8 * order**3,
        )
        mode_high, mode_low = call(
            coarse_body(modes, edge, cases, devices), "coarse_map",
            [((order, total), BF16)] * 2, (*payloads, *got),
        )

        def jump(mine, his):
            return jnp.concatenate([a[:edge, :] - b[:edge, :] for a, b in zip(mine, his)], axis=0)

        def put(outs, x):
            for k, out in enumerate(outs):
                out[...] = x[k * edge : (k + 1) * edge]

        def gathered(ref):
            return jnp.concatenate([ref[:, m, :] for m in range(modes)], axis=0)

        edges = [((edge, cases), F32)] * 4
        field = [((order, cases), F32)]

        def second(*refs):
            mine, his = refs[0:4], refs[4:8]
            high, low, pick, residual_out = refs[8:12]
            outs, sent = refs[12:16], refs[16]
            residual = jump(mine, his)
            residual_out[...] = residual
            put(outs, 0.25 * dot_split(high[...], low[...], residual))
            sent[...] = jnp.broadcast_to(
                dot_exact(pick[...].astype(BF16), residual)[None, :modes], sent.shape
            )

        residual, *lifted, sent = call(
            second, "apply_precond_0", field + edges + [((devices, modes, cases), F32)],
            (*payloads, *got, pre_high, pre_low, corner), 3 * mat,
        )
        got = swap(lifted)
        coarse = to_all(sent)

        def third(*refs):
            mine, his = refs[0:4], refs[4:8]
            coarse, m_high, m_low, high, low, search_out = refs[8:14]
            search = jump(mine, his) + dot_split(m_high[...], m_low[...], gathered(coarse))
            search_out[...] = search
            put(refs[14:18], dot_split(high[...], low[...], search))

        search, *image = call(
            third, "apply_schur_0", field + edges,
            (*lifted, *got, coarse, mode_high, mode_low, sch_high, sch_low), 3 * mat,
        )
        got = swap(image)

        def fourth(*refs):
            mine, his = refs[0:4], refs[4:8]
            residual, search, high, low, pick, dual_out = refs[8:14]
            outs, sent = refs[14:18], refs[18]
            dual = jump(mine, his)
            dual_out[...] = dual
            put(outs, 0.25 * dot_split(high[...], low[...], dual))
            rows = [
                dot_exact(pick[...].astype(BF16), dual)[:modes],
                jnp.sum(residual[...] * search[...], axis=0, keepdims=True),
                jnp.sum(search[...] * dual, axis=0, keepdims=True),
            ]
            sent[...] = jnp.broadcast_to(jnp.concatenate(rows, axis=0)[None], sent.shape)

        dual, *lifted, sent = call(
            fourth, "apply_precond_1", field + edges + [((devices, modes + 2, cases), F32)],
            (*image, *got, residual, search, pre_high, pre_low, corner), 3 * mat,
        )
        got = swap(lifted)
        coarse = to_all(sent)

        def fifth(*refs):
            mine, his = refs[0:4], refs[4:8]
            coarse, m_high, m_low, high, low = refs[8:13]
            image = refs[13:17]
            residual, search, dual, next_out, step_out = refs[17:22]
            outs, sent = refs[22:26], refs[26]
            change = jump(mine, his) + dot_split(m_high[...], m_low[...], gathered(coarse))
            change_image = dot_split(high[...], low[...], change)
            put(outs, change_image)
            step = jnp.sum(coarse[:, modes, :], axis=0, keepdims=True) / jnp.sum(
                coarse[:, modes + 1, :], axis=0, keepdims=True
            )
            step_out[...] = step
            following = search[...] - step * change
            next_out[...] = following
            schur_image = jnp.concatenate([x[...] for x in image], axis=0) - step * change_image
            rows = [
                jnp.sum((residual[...] - step * dual[...]) * following, axis=0, keepdims=True),
                2.0 * jnp.sum(following * schur_image, axis=0, keepdims=True),
            ]
            sent[...] = jnp.broadcast_to(jnp.concatenate(rows, axis=0)[None], sent.shape)

        following, step, *change_image, sent = call(
            fifth, "apply_schur_1",
            field + [((1, cases), F32)] + edges + [((devices, 2, cases), F32)],
            (*lifted, *got, coarse, mode_high, mode_low, sch_high, sch_low, *image,
             residual, search, dual), 3 * mat,
        )
        got = swap(change_image)
        sums = to_all(sent)

        def last(*refs):
            mine, his = refs[0:4], refs[4:8]
            sums, step, rows_row, residual, search, dual, following, mult_out, res_out = refs[8:]
            back = one_hot_cols(rows_row[...], order)
            step, dual = step[...], dual[...]
            final = jnp.sum(sums[:, 0, :], axis=0, keepdims=True) / jnp.sum(
                sums[:, 1, :], axis=0, keepdims=True
            )
            mult_out[...] = dot_exact(back, step * search[...] + final * following[...])
            new_dual = dual - step * jump(mine, his)
            res_out[...] = dot_exact(back, residual[...] - step * dual - final * new_dual)

        multipliers, residual = call(
            last, "finish", field * 2,
            (*change_image, *got, sums, step, rows_row, residual, search, dual, following), 6 * mat,
        )
        return multipliers[None, None], residual[None, None]

    in_specs = (
        P("gx", "gy", None, None),
        P("gx", "gy", None, None),
        P("gx", "gy", None, None),
        P("gx", None),
        P("gx", "gy", None),
        P("gx", "gy", None),
    )
    out_specs = (P("gx", "gy", None, None), P("gx", "gy", None, None))
    return jax.shard_map(
        on_device, mesh=mesh, in_specs=in_specs, out_specs=out_specs, check_vma=False
    )
```
